32 devices in a mesh: dp: 16 (over z, y, core), seq: 2 (over x).
Axes of the slice: x: 2, y: 2, z: 4, core: 2. Of those that a mesh axis runs over, the one named last changes fastest.
Arguments:
- block_input: bfloat16 [16, 256, 1088], P('dp', 'seq'), may hold values from -6 to 6
- grad_output: bfloat16 [16, 256, 1088], P('dp', 'seq'), may hold values from -6 to 6
- segments: int32 [16, 256], P('dp'), may hold values from 0 to 2, never falling along the last dimension, each value on 1 to 128 neighbouring positions
- w_qkv: bfloat16 [32, 110976], P(('dp', 'seq')), as said below
- w_out: bfloat16 [32, 36992], P(('dp', 'seq')), may hold values from -0.5 to 0.5
- w_fc1: bfloat16 [32, 147968], P(('dp', 'seq')), may hold values from -0.1875 to 0.1875
- w_fc2: bfloat16 [32, 147968], P(('dp', 'seq')), may hold values from -0.09375 to 0.09375
- params: bfloat16 [32, 408], P(('dp', 'seq')), may hold values from -2 to 2, as said below
Outputs:
- block_output: bfloat16 [16, 256, 1088], P('dp', 'seq')
- grad_input: float32 [16, 256, 1088], P('dp', 'seq')
- grad_qkv: float32 [32, 110976], P(('dp', 'seq'))
- grad_out: float32 [32, 36992], P(('dp', 'seq'))
- grad_fc1: float32 [32, 147968], P(('dp', 'seq'))
- grad_fc2: float32 [32, 147968], P(('dp', 'seq'))
- grad_params: float32 [32, 408], P(('dp', 'seq'))
The draws below stay inside these ranges and needn't reach their ends.
Inputs may be any that keep to these rules, and one draw needn't show every extreme that they name: `segments`: segment numbers never fall along a sequence and start at 0; each document holds 1 to 128 positions, and one holds exactly that many. `w_qkv`: entries of a matrix of fan-in 1088. `params`: both norms' gains lie in 0.5 to 1.5; every bias lies in -2 to 2.
All inputs are finite; a program needn't handle non-finite values.
Results may differ from the reference program's by a relative error of at most 0.0095.
Values may be sent and summed in bfloat16 or wider, within the bound.
A program may use at most 256 MiB of HBM per device.

```python
import math
import jax
import jax.numpy as jnp
import numpy as np
from jax import lax

HEADS = 17
HEAD_DIM = 64
FF = 4352
D = 1088
SEQ_LEN = 256
BATCH = 16
NVEC = 13056
DOCS = 3
DEVICES = 32


def draw_w_qkv(key, part):
    base = jax.random.normal(key, (D, 3 * D), jnp.float32) * D ** (-0.5)
    return base.reshape(DEVICES, 3 * D * D // DEVICES).astype(jnp.bfloat16)


def draw_params(key, part):
    index = jnp.arange(8 * D + FF)
    gain_slot = (index < D) | (index >= 5 * D) & (index < 6 * D)
    gains = jax.random.uniform(jax.random.fold_in(key, 1), (8 * D + FF,), jnp.float32, 0.5, 1.5)
    shifts = jnp.clip(jax.random.normal(jax.random.fold_in(key, 2), (8 * D + FF,), jnp.float32) * 0.5, -2.0, 2.0)
    return jnp.where(gain_slot, gains, shifts).reshape(DEVICES, (8 * D + FF) // DEVICES).astype(jnp.bfloat16)


def level_of(stream_key, extent, cuts, low, high):
    loudness = 1.0
    for position, parts in cuts:
        heights = jax.random.uniform(jax.random.fold_in(jax.random.fold_in(stream_key, 6), position), (parts,), jnp.float32, low / len(cuts), high / len(cuts))
        loudness = loudness * jnp.repeat(jnp.exp(heights), extent[position] // parts).reshape((-1,) + (1,) * (len(extent) - 1 - position))
    return loudness


def split_up(count, total, reach, lean):
    portions = [(1 << 20) // math.isqrt(standing ** lean) + 1 for standing in range(2, count + 1)]
    rest, given = total - reach - (count - 1), [1] * (count - 1)
    while rest > 0:
        candidates = [i for i in range(count - 1) if given[i] < reach]
        whole, left = sum([portions[i] for i in candidates]), rest
        for i in candidates:
            addition = min(reach - given[i], max(1, left * portions[i] // whole), rest)
            given[i] = given[i] + addition
            rest = rest - addition
    return np.array([reach] + given)


def ragged(key, count, total, most, lean):
    if count == 2:
        one = jax.random.randint(key, (), max(1, total - most), min(most, total - 1) + 1)
        return jnp.stack([one, total - one])
    lengths = jnp.asarray(split_up(count, total, most, lean), jnp.int32)
    couples = (count - 1) // 2
    donor, sink = lengths[1:1 + 2 * couples:2], lengths[2:2 + 2 * couples:2]
    margin = jnp.minimum(donor - 1, most - sink)
    passed = jax.random.randint(jax.random.fold_in(key, 1), (couples,), 0, 1 << 20) % (margin + 1)
    lengths = lengths.at[1:1 + 2 * couples:2].set(donor - passed).at[2:2 + 2 * couples:2].set(sink + passed)
    return lengths[jax.random.permutation(jax.random.fold_in(key, 2), count)]


def gaussian(rng, shape, width, most, cuts=(), kind=jnp.bfloat16):
    drawn = jax.random.normal(rng, shape, jnp.float32) * width
    if len(cuts) > 0:
        drawn = level_of(rng, shape, cuts, -0.22, 0.18) * drawn
    return jnp.clip(drawn, min=-most, max=most).astype(kind)


def setup_inputs(seed: int = 0) -> dict:
    key_of = jax.random.split(jax.random.key(seed), 9)
    block_input = gaussian(key_of[0], (BATCH, SEQ_LEN, D), 1.0, 6.0, ((0, 16), (1, 2)))
    grad_output = gaussian(key_of[1], (BATCH, SEQ_LEN, D), 1.0, 6.0, ((0, 16), (1, 2)))
    segments = jax.vmap(lambda own: jnp.searchsorted(jnp.cumsum(ragged(own, DOCS, SEQ_LEN, SEQ_LEN // 2, 0)), jnp.arange(SEQ_LEN), side="right"))(jax.random.split(key_of[2], BATCH)).reshape((BATCH, SEQ_LEN)).astype(jnp.int32)
    w_qkv = draw_w_qkv(jax.random.fold_in(key_of[8], 71), 0)
    w_out = gaussian(key_of[4], (DEVICES, D * D // DEVICES), (D // 8) ** -0.5, 0.5, ((0, 32),))
    w_fc1 = gaussian(key_of[5], (DEVICES, D * FF // DEVICES), D ** -0.5, 0.1875, ((0, 32),))
    w_fc2 = gaussian(key_of[6], (DEVICES, FF * D // DEVICES), FF ** -0.5, 0.09375, ((0, 32),))
    params = draw_params(jax.random.fold_in(key_of[8], 71), 0)
    return {"block_input": block_input, "grad_output": grad_output, "segments": segments, "w_qkv": w_qkv, "w_out": w_out, "w_fc1": w_fc1, "w_fc2": w_fc2, "params": params}


EPS = 1e-05
SCALE = 0.125
GELU_C = 0.7978845608028654
CUBIC = 0.044715

def layer_norm(rows, gain, shift):
    mean = lax.optimization_barrier(jnp.mean(rows, axis=-1, keepdims=True))
    centred = rows - mean
    var = lax.optimization_barrier(jnp.mean(centred * centred, axis=-1, keepdims=True))
    inv_std = lax.rsqrt(var + EPS)
    normed = centred * inv_std
    return (normed * gain + shift, normed, inv_std)

def norm_back(upstream, normed, inv_std, gain):
    scaled = upstream * gain
    return inv_std * (scaled - lax.optimization_barrier(jnp.mean(scaled, axis=-1, keepdims=True)) - normed * lax.optimization_barrier(jnp.mean(scaled * normed, axis=-1, keepdims=True)))

def gelu_value(u):
    inner = GELU_C * (u + CUBIC * u * u * u)
    return 0.5 * u * (1.0 + jnp.tanh(inner))

def gelu_slope(u):
    tval = jnp.tanh(GELU_C * (u + CUBIC * u * u * u))
    return 0.5 * (1.0 + tval) + 0.5 * u * (1.0 - tval * tval) * GELU_C * (1.0 + 3.0 * CUBIC * u * u)

def split_params(vec):
    whole = vec.reshape(-1).astype(jnp.float32)
    pieces = []
    start = 0
    for length in [D, D, D, D, D, D, D, FF, D]:
        pieces.append(whole[start:start + length])
        start = start + length
    return pieces

def widen(value):
    return lax.optimization_barrier(value.astype(jnp.bfloat16)).astype(jnp.float32)

def scores_of(query, keys, allowed):
    raw = jnp.einsum('brhe,bshe->bhrs', query.astype(jnp.float32), keys.astype(jnp.float32)) * SCALE
    return jnp.where(allowed[:, None], raw, -1e+30)

def attend_forward(query, keys, values, allowed):
    scores = scores_of(query, keys, allowed)
    top = lax.optimization_barrier(jnp.max(scores, axis=-1, keepdims=True))
    lse = top + jnp.log(lax.optimization_barrier(jnp.sum(jnp.exp(scores - top), axis=-1, keepdims=True)))
    prob = jnp.exp(scores - lse)
    out = jnp.einsum('bhrs,bshe->brhe', widen(prob), values.astype(jnp.float32))
    return (out.astype(jnp.bfloat16), lse)

def attend_back(query, keys, values, out, dout, lse, allowed):
    scores = scores_of(query, keys, allowed)
    prob = jnp.exp(scores - lse)
    dout_f = dout.astype(jnp.float32)
    dvals = jnp.einsum('bhrs,brhe->bshe', widen(prob), dout_f)
    dprob = jnp.einsum('brhe,bshe->bhrs', dout_f, values.astype(jnp.float32))
    delta = lax.optimization_barrier(jnp.sum(dout_f * out.astype(jnp.float32), axis=-1))
    delta = jnp.transpose(delta, (0, 2, 1))[..., None]
    dscore = widen(prob * (dprob - delta) * SCALE)
    dquery = jnp.einsum('bhrs,bshe->brhe', dscore, keys.astype(jnp.float32))
    dkeys = jnp.einsum('bhrs,brhe->bshe', dscore, query.astype(jnp.float32))
    return (dquery, dkeys, dvals)

def reference(block_input, grad_output, segments, w_qkv, w_out, w_fc1, w_fc2, params):
    mat_qkv = w_qkv.reshape(D, 3 * D)
    mat_out = w_out.reshape(D, D)
    mat_fc1 = w_fc1.reshape(D, FF)
    mat_fc2 = w_fc2.reshape(FF, D)
    gain1, shift1, bias_q, bias_v, bias_o, gain2, shift2, bias_f1, bias_f2 = split_params(params)
    bias_qkv = jnp.concatenate([bias_q, jnp.zeros((D,), jnp.float32), bias_v])
    f32 = jnp.float32

    def one_sequence(totals, item):
        inputs, cotangent, segs = item
        rows = inputs.astype(f32)
        h1f, normed1, inv1 = layer_norm(rows, gain1, shift1)
        h1 = h1f.astype(jnp.bfloat16)
        qkv = (jnp.dot(h1, mat_qkv, preferred_element_type=f32) + bias_qkv).astype(jnp.bfloat16)
        query = qkv[:, :D].reshape(1, SEQ_LEN, HEADS, HEAD_DIM)
        keys = qkv[:, D:2 * D].reshape(1, SEQ_LEN, HEADS, HEAD_DIM)
        values = qkv[:, 2 * D:].reshape(1, SEQ_LEN, HEADS, HEAD_DIM)
        places = jnp.arange(SEQ_LEN, dtype=jnp.int32)
        allowed = ((segs[:, None] == segs[None, :]) & (places[None, :] <= places[:, None]))[None]
        out, lse = attend_forward(query, keys, values, allowed)
        out_rows = out.reshape(SEQ_LEN, D)
        resid = rows + jnp.dot(out_rows, mat_out, preferred_element_type=f32) + bias_o
        h2f, normed2, inv2 = layer_norm(resid, gain2, shift2)
        h2 = h2f.astype(jnp.bfloat16)
        upper = jnp.dot(h2, mat_fc1, preferred_element_type=f32) + bias_f1
        act = gelu_value(upper).astype(jnp.bfloat16)
        result = (resid + jnp.dot(act, mat_fc2, preferred_element_type=f32) + bias_f2).astype(jnp.bfloat16)
        cot_f = cotangent.astype(f32)
        d_fc2 = jnp.dot(act.T, cotangent, preferred_element_type=f32)
        d_bf2 = lax.optimization_barrier(jnp.sum(cot_f, axis=0))
        d_upper = jnp.dot(cotangent, mat_fc2.T, preferred_element_type=f32) * gelu_slope(upper)
        d_bf1 = lax.optimization_barrier(jnp.sum(d_upper, axis=0))
        d_upper_b = d_upper.astype(jnp.bfloat16)
        d_fc1 = jnp.dot(h2.T, d_upper_b, preferred_element_type=f32)
        d_h2 = jnp.dot(d_upper_b, mat_fc1.T, preferred_element_type=f32)
        d_gain2 = lax.optimization_barrier(jnp.sum(d_h2 * normed2, axis=0))
        d_shift2 = lax.optimization_barrier(jnp.sum(d_h2, axis=0))
        d_resid = cot_f + norm_back(d_h2, normed2, inv2, gain2)
        d_resid_b = d_resid.astype(jnp.bfloat16)
        d_out = jnp.dot(out_rows.T, d_resid_b, preferred_element_type=f32)
        d_bo = lax.optimization_barrier(jnp.sum(d_resid, axis=0))
        d_attn = jnp.dot(d_resid_b, mat_out.T, preferred_element_type=f32).astype(jnp.bfloat16)
        d_attn = d_attn.reshape(1, SEQ_LEN, HEADS, HEAD_DIM)
        dquery, dkeys, dvals = attend_back(query, keys, values, out, d_attn, lse, allowed)
        dquery = dquery.reshape(SEQ_LEN, D)
        dkeys = dkeys.reshape(SEQ_LEN, D)
        dvals = dvals.reshape(SEQ_LEN, D)
        d_qkv_b = jnp.concatenate([dquery, dkeys, dvals], axis=1).astype(jnp.bfloat16)
        d_qkv = jnp.dot(h1.T, d_qkv_b, preferred_element_type=f32)
        d_bq = lax.optimization_barrier(jnp.sum(dquery, axis=0))
        d_bv = lax.optimization_barrier(jnp.sum(dvals, axis=0))
        d_h1 = jnp.dot(d_qkv_b, mat_qkv.T, preferred_element_type=f32)
        d_gain1 = lax.optimization_barrier(jnp.sum(d_h1 * normed1, axis=0))
        d_shift1 = lax.optimization_barrier(jnp.sum(d_h1, axis=0))
        d_input = d_resid + norm_back(d_h1, normed1, inv1, gain1)
        d_vec = jnp.concatenate([d_gain1, d_shift1, d_bq, d_bv, d_bo, d_gain2, d_shift2, d_bf1, d_bf2])
        totals = (totals[0] + d_qkv, totals[1] + d_out, totals[2] + d_fc1, totals[3] + d_fc2, totals[4] + d_vec)
        return (totals, (result, d_input))
    start = (jnp.zeros((D, 3 * D), jnp.float32), jnp.zeros((D, D), jnp.float32), jnp.zeros((D, FF), jnp.float32), jnp.zeros((FF, D), jnp.float32), jnp.zeros((NVEC,), jnp.float32))
    totals, (outputs, grads_in) = lax.scan(one_sequence, start, (block_input, grad_output, segments))
    return (outputs, grads_in, totals[0].reshape(DEVICES, -1), totals[1].reshape(DEVICES, -1), totals[2].reshape(DEVICES, -1), totals[3].reshape(DEVICES, -1), totals[4].reshape(DEVICES, -1))
```

```python
import functools

import jax
import jax.numpy as jnp
from jax import lax
from jax.experimental import pallas as pl
from jax.experimental.pallas import tpu as pltpu
from jax.sharding import PartitionSpec as P

HEADS = 17
HEAD_DIM = 64
FF = 4352
D = 1088


EPS = 1e-05
SCALE = 0.125
GELU_C = 0.7978845608028654
CUBIC = 0.044715
AXES = ("dp", "seq")


def layer_norm(rows, gain, shift):
    mean = jnp.mean(rows, axis=-1, keepdims=True)
    centred = rows - mean
    var = jnp.mean(centred * centred, axis=-1, keepdims=True)
    inv_std = lax.rsqrt(var + EPS)
    normed = centred * inv_std
    return (normed * gain + shift, normed, inv_std)


def norm_back(upstream, normed, inv_std, gain):
    scaled = upstream * gain
    return inv_std * (
        scaled
        - jnp.mean(scaled, axis=-1, keepdims=True)
        - normed * jnp.mean(scaled * normed, axis=-1, keepdims=True)
    )


def gelu_value(u):
    inner = GELU_C * (u + CUBIC * u * u * u)
    return 0.5 * u * (1.0 + jnp.tanh(inner))


def gelu_slope(u):
    tval = jnp.tanh(GELU_C * (u + CUBIC * u * u * u))
    return 0.5 * (1.0 + tval) + 0.5 * u * (1.0 - tval * tval) * GELU_C * (1.0 + 3.0 * CUBIC * u * u)


def split_params(vec):
    whole = vec.reshape(-1).astype(jnp.float32)
    pieces = []
    start = 0
    for length in [D, D, D, D, D, D, D, FF, D]:
        pieces.append(whole[start : start + length])
        start = start + length
    return pieces


def scores_of(query, keys, allowed):
    raw = jnp.einsum("brhe,bshe->bhrs", query, keys, preferred_element_type=jnp.float32) * SCALE
    return jnp.where(allowed[:, None], raw, -1e30)


def attend_forward(query, keys, values, allowed):
    scores = scores_of(query, keys, allowed)
    top = jnp.max(scores, axis=-1, keepdims=True)
    lse = top + jnp.log(jnp.sum(jnp.exp(scores - top), axis=-1, keepdims=True))
    prob = jnp.exp(scores - lse).astype(jnp.bfloat16)
    out = jnp.einsum("bhrs,bshe->brhe", prob, values, preferred_element_type=jnp.float32)
    return (out.astype(jnp.bfloat16), lse)


def attend_back(query, keys, values, out, dout, lse, allowed):
    scores = scores_of(query, keys, allowed)
    prob = jnp.exp(scores - lse)
    dvals = jnp.einsum(
        "bhrs,brhe->bshe", prob.astype(jnp.bfloat16), dout, preferred_element_type=jnp.float32
    )
    dprob = jnp.einsum("brhe,bshe->bhrs", dout, values, preferred_element_type=jnp.float32)
    delta = jnp.sum(dout.astype(jnp.float32) * out.astype(jnp.float32), axis=-1)
    delta = jnp.transpose(delta, (0, 2, 1))[..., None]
    dscore = (prob * (dprob - delta) * SCALE).astype(jnp.bfloat16)
    dquery = jnp.einsum("bhrs,bshe->brhe", dscore, keys, preferred_element_type=jnp.float32)
    dkeys = jnp.einsum("bhrs,brhe->bshe", dscore, query, preferred_element_type=jnp.float32)
    return (dquery, dkeys, dvals)


def piece_rows(shard, cols):
    piece, count = shard.shape[1], lax.axis_size(AXES)
    return piece // cols if piece % cols == 0 and count & (count - 1) == 0 else 0


def column_order(rows, devices, held):
    main = held // 8 * 8
    rest = held - main
    place = jnp.arange(rows, dtype=jnp.int32)
    owner, inner = place // held, place % held
    target = jnp.where(inner < main, owner * main + inner, devices * main + owner * rest + inner - main)
    return (target[:, None] == place[None, :]).astype(jnp.bfloat16)


def bit_order(count, flip):
    bits = list(range((count - 1).bit_length()))
    first = bits[1:2] + bits[:1] + bits[2:3]
    if flip and len(first) == 3:
        first = [first[0], first[2], first[1]]
    return first + bits[:2:-1]


def swap(value, bit):
    count = lax.axis_size(AXES)
    return lax.ppermute(value, AXES, [(i, i ^ (1 << bit)) for i in range(count)])


def sum_by_halves(block, flip):
    rank = lax.axis_index(AXES)
    known = list(range((block.shape[0] - 1).bit_length()))
    tail = block.shape[1:]
    acc = block
    for bit in bit_order(block.shape[0], flip):
        low = known.index(bit)
        high = len(known) - 1 - low
        view = acc.reshape((1 << high, 2, 1 << low) + tail)
        mine = (rank >> bit) & 1
        send = lax.dynamic_index_in_dim(view, 1 - mine, 1, keepdims=False).astype(block.dtype)
        keep = lax.dynamic_index_in_dim(view, mine, 1, keepdims=False).astype(jnp.float32)
        acc = keep + swap(send, bit).astype(jnp.float32)
        known.remove(bit)
    return acc.reshape(tail)


def gather_by_doubling(local, flip):
    count = lax.axis_size(AXES)
    rank = lax.axis_index(AXES)
    rows, cols = local.shape
    known = []
    acc = local[None]
    for bit in reversed(bit_order(count, flip)):
        low = sum(other < bit for other in known)
        high = len(known) - low
        other = swap(acc, bit).reshape(1 << high, 1 << low, rows, cols)
        own = acc.reshape(1 << high, 1 << low, rows, cols)
        mine = ((rank >> bit) & 1) == 1
        acc = jnp.stack([jnp.where(mine, other, own), jnp.where(mine, own, other)], axis=1)
        acc = acc.reshape(-1, rows, cols)
        known.append(bit)
    return acc.reshape(count * rows, cols)


def gather_matrices(shards, shapes, flips):
    whole = []
    rests = []
    for shard, (rows, cols), flip in zip(shards, shapes, flips):
        held = piece_rows(shard, cols)
        if held == 0:
            full = lax.all_gather(shard, AXES, axis=0, tiled=True)
            whole.append([full.reshape(rows, cols)])
            continue
        local = shard.reshape(held, cols)
        main = held // 8 * 8
        whole.append([gather_by_doubling(local[:main], flip)] if main else [])
        if held - main:
            rests.append((whole[-1], local[main:]))
    for extra in sorted({rest.shape[0] for _, rest in rests}):
        same = [(parts, rest) for parts, rest in rests if rest.shape[0] == extra]
        joined = gather_by_doubling(jnp.concatenate([rest for _, rest in same], axis=1), True)
        start = 0
        for parts, rest in same:
            parts.append(joined[:, start : start + rest.shape[1]])
            start += rest.shape[1]
    return whole


def gather_seq(local):
    if lax.axis_size("seq") != 2:
        return lax.all_gather(local, "seq", axis=1, tiled=True)
    other = lax.ppermute(local, "seq", [(0, 1), (1, 0)])
    late = lax.axis_index("seq") == 1
    return jnp.concatenate([jnp.where(late, other, local), jnp.where(late, local, other)], axis=1)


def scatter_seq(terms):
    if lax.axis_size("seq") != 2:
        return lax.psum_scatter(terms, "seq", scatter_dimension=1, tiled=True)
    toks = terms.shape[1] // 2
    place = lax.axis_index("seq")
    send = lax.dynamic_slice_in_dim(terms, (1 - place) * toks, toks, 1)
    keep = lax.dynamic_slice_in_dim(terms, place * toks, toks, 1)
    return keep + lax.ppermute(send, "seq", [(0, 1), (1, 0)])


def times(left, parts, bias=None):
    total = 0.0
    start = 0
    for part in parts:
        total = total + jnp.dot(
            left[:, start : start + part.shape[0]], part, preferred_element_type=jnp.float32
        )
        start += part.shape[0]
    return total


def times_t(left, parts):
    return jnp.concatenate(
        [
            lax.dot_general(left, part, (((1,), (1,)), ((), ())), preferred_element_type=jnp.float32)
            for part in parts
        ],
        axis=1,
    )


def grad_block(left, right):
    return lax.dot_general(left, right, (((0,), (0,)), ((), ())), preferred_element_type=jnp.float32)


def scatter_grad(left, right, parts, shard, flip):
    count = lax.axis_size(AXES)
    cols = right.shape[1]
    held = piece_rows(shard, cols)
    if held == 0:
        block = grad_block(left, right).reshape(count, shard.shape[1])
        return lax.psum_scatter(block, AXES, scatter_dimension=0, tiled=True), None
    main = held // 8 * 8
    top = rest = None
    if main:
        block = grad_block(left[:, : count * main], right).astype(jnp.bfloat16)
        top = sum_by_halves(block.reshape(count, main, cols), flip)
    if held - main:
        rest = grad_block(left[:, count * main :], right).astype(jnp.bfloat16)
        rest = rest.reshape(count, held - main, cols)
    return top, rest


def finish_grads(pairs, shards):
    rests = [rest for _, rest in pairs if rest is not None]
    summed = {}
    for extra in sorted({rest.shape[1] for rest in rests}):
        group = [i for i, (_, rest) in enumerate(pairs) if rest is not None and rest.shape[1] == extra]
        joined = sum_by_halves(jnp.concatenate([pairs[i][1] for i in group], axis=2), True)
        start = 0
        for i in group:
            cols = pairs[i][1].shape[2]
            summed[i] = joined[:, start : start + cols]
            start += cols
    grads = []
    for i, ((top, _), shard) in enumerate(zip(pairs, shards)):
        rows = [part for part in (top, summed.get(i)) if part is not None]
        grads.append(jnp.concatenate(rows, axis=0).reshape(shard.shape))
    return grads


def reorder(values, order):
    if order is None:
        return values
    return jnp.dot(values, order, preferred_element_type=jnp.float32).astype(values.dtype)


def restore(values, order):
    if order is None:
        return values
    return lax.dot_general(
        values,
        order.astype(values.dtype),
        (((1,), (1,)), ((), ())),
        precision=lax.Precision.HIGHEST if values.dtype == jnp.float32 else None,
        preferred_element_type=jnp.float32,
    ).astype(values.dtype)


MESH = pl.DeviceIdType.MESH


class Place:
    def __init__(self, depth):
        self.depth = depth
        dp, self.x = lax.axis_index("dp"), lax.axis_index("seq")
        self.core = lax.rem(dp, 2)
        self.y = lax.rem(lax.div(dp, 2), 2)
        self.z = lax.div(dp, 4)
        self.near = self.core * self.y + (1 - self.core) * self.x
        self.far = self.core * self.x + (1 - self.core) * self.y

    def at(self, z, near, far, core=None):
        mine = self.core if core is None else core
        y = self.core * near + (1 - self.core) * far
        x = self.core * far + (1 - self.core) * near
        return ((z * 2 + y) * 2 + mine, x)

    def group(self, near, far):
        y = self.core * near + (1 - self.core) * far
        x = self.core * far + (1 - self.core) * near
        return y * 2 + x

    def neighbours(self):
        fixed = [
            self.at(self.z, 1 - self.near, self.far),
            self.at(self.z, self.near, 1 - self.far),
            self.at(self.z, self.near, self.far, 1 - self.core),
        ]
        return fixed, self.at(self.z + 1, self.near, self.far), self.at(self.z - 1, self.near, self.far)

    def meet(self):
        fixed, above, below = self.neighbours()
        barrier = pltpu.get_barrier_semaphore()
        for other in fixed:
            pl.semaphore_signal(barrier, inc=1, device_id=other, device_id_type=MESH)

        @pl.when(self.z + 1 < self.depth)
        def _():
            pl.semaphore_signal(barrier, inc=1, device_id=above, device_id_type=MESH)

        @pl.when(self.z > 0)
        def _():
            pl.semaphore_signal(barrier, inc=1, device_id=below, device_id_type=MESH)

        low, high = self.z == 0, self.z == self.depth - 1

        @pl.when(jnp.logical_not(low | high))
        def _():
            pl.semaphore_wait(barrier, 5)

        @pl.when(low != high)
        def _():
            pl.semaphore_wait(barrier, 4)

        @pl.when(low & high)
        def _():
            pl.semaphore_wait(barrier, 3)


def gather_kernel(depth, natural, *refs):
    pieces = len(natural)
    ins, outs = refs[:pieces], refs[pieces : 2 * pieces]
    local_sem, arrive, from_core, up_sem, down_sem, pair_sem = refs[2 * pieces :]
    place = Place(depth)
    z, near, far, core = place.z, place.near, place.far, place.core
    (to_near, to_far, to_core), above, below = place.neighbours()
    place.meet()
    all_pieces = range(pieces)

    def slot(zb, a, b):
        return place.group(a, b) * depth + zb

    def block(p, index):
        if natural[p]:
            group, zb = lax.div(index, depth), lax.rem(index, depth)
            y, x = lax.div(group, 2), lax.rem(group, 2)
            return outs[p].at[((zb * 2 + y) * 2 + core) * 2 + x]
        return outs[p].at[core * (4 * depth) + index]

    def send(p, src, index, sem, target, recv=None):
        pltpu.make_async_remote_copy(
            src_ref=src,
            dst_ref=block(p, index),
            send_sem=sem,
            recv_sem=arrive.at[index, p] if recv is None else recv,
            device_id=target,
            device_id_type=MESH,
        ).start()

    def wait_block(p, index):
        pltpu.make_async_copy(ins[p], block(p, index), arrive.at[index, p]).wait()

    def spread(p, src, zb):
        index = slot(zb, near, far)
        send(p, src, index, pair_sem.at[0, p], to_near)
        send(p, src, index, pair_sem.at[1, p], to_far)
        send(p, src, index, pair_sem.at[2, p], to_core, from_core.at[p])

    own = slot(z, near, far)
    for p in all_pieces:
        @pl.when(z + 1 < depth)
        def _():
            send(p, ins[p], own, up_sem.at[0, p], above)

        @pl.when(z > 0)
        def _():
            send(p, ins[p], own, down_sem.at[0, p], below)

        spread(p, ins[p], z)
        pltpu.make_async_copy(ins[p], block(p, own), local_sem.at[p]).start()

    def from_near(zb):
        index = slot(zb, 1 - near, far)
        for p in all_pieces:
            wait_block(p, index)
            send(p, block(p, index), index, pair_sem.at[1, p], to_far)
            send(p, block(p, index), index, pair_sem.at[2, p], to_core, from_core.at[p])

    from_near(z)
    for d in range(1, depth):
        @pl.when(z >= d)
        def _():
            index = slot(z - d, near, far)
            for p in all_pieces:
                wait_block(p, index)

                @pl.when(z + 1 < depth)
                def _():
                    send(p, block(p, index), index, up_sem.at[d, p], above)

                spread(p, block(p, index), z - d)

        @pl.when(z + d < depth)
        def _():
            index = slot(z + d, near, far)
            for p in all_pieces:
                wait_block(p, index)

                @pl.when(z > 0)
                def _():
                    send(p, block(p, index), index, down_sem.at[d, p], below)

                spread(p, block(p, index), z + d)

        @pl.when(z >= d)
        def _():
            from_near(z - d)

        @pl.when(z + d < depth)
        def _():
            from_near(z + d)

    def from_far(zb, a):
        index = slot(zb, a, 1 - far)
        for p in all_pieces:
            wait_block(p, index)
            send(p, block(p, index), index, pair_sem.at[2, p], to_core, from_core.at[p])

    for d in range(depth):
        for a in (near, 1 - near):
            @pl.when(z >= d)
            def _():
                from_far(z - d, a)

            if d > 0:
                @pl.when(z + d < depth)
                def _():
                    from_far(z + d, a)

    for p in all_pieces:
        pltpu.make_async_copy(ins[p], block(p, own), local_sem.at[p]).wait()
        for d in range(depth):
            @pl.when((z >= d) & (z + 1 < depth))
            def _():
                pltpu.make_async_copy(ins[p], block(p, own), up_sem.at[d, p]).wait()

            @pl.when((z + d < depth) & (z > 0))
            def _():
                pltpu.make_async_copy(ins[p], block(p, own), down_sem.at[d, p]).wait()

        for kind, size in ((0, depth), (1, 2 * depth), (2, 4 * depth)):
            some = outs[p].at[pl.ds(0, size)]
            pltpu.make_async_copy(some, some, pair_sem.at[kind, p]).wait()
        some = outs[p].at[pl.ds(0, 4 * depth)]
        pltpu.make_async_copy(some, some, from_core.at[p]).wait()


def gather_all(blocks, natural, depth):
    pieces = len(blocks)
    count = 8 * depth
    return pl.pallas_call(
        functools.partial(gather_kernel, depth, natural),
        out_shape=[jax.ShapeDtypeStruct((count,) + block.shape, block.dtype) for block in blocks],
        in_specs=[pl.BlockSpec(memory_space=pltpu.VMEM)] * pieces,
        out_specs=[pl.BlockSpec(memory_space=pltpu.HBM)] * pieces,
        scratch_shapes=[
            pltpu.SemaphoreType.DMA((pieces,)),
            pltpu.SemaphoreType.DMA((4 * depth, pieces)),
            pltpu.SemaphoreType.DMA((pieces,)),
            pltpu.SemaphoreType.DMA((depth, pieces)),
            pltpu.SemaphoreType.DMA((depth, pieces)),
            pltpu.SemaphoreType.DMA((3, pieces)),
        ],
        compiler_params=pltpu.CompilerParams(collective_id=0, has_side_effects=True, vmem_limit_bytes=16 << 20),
        name="gather_all",
    )(*blocks)


def reduce_kernel(depth, dots, pieces, *refs):
    refs = list(refs)

    def take(count):
        taken = refs[:count]
        del refs[:count]
        return taken

    lefts, rights, givens = take(dots), take(dots), take(pieces - dots)
    outs, work, core_in, far_in, near_in, up_in, down_in = (take(pieces) for _ in range(7))
    core_out, core_got, far_out, far_got, near_out, near_got, up_out, up_got, down_out, down_got = refs
    place = Place(depth)
    z, near, far, core = place.z, place.near, place.far, place.core
    (to_near, to_far, to_core), above, below = place.neighbours()
    place.meet()
    f32 = jnp.float32
    here, beside = place.group(near, far), place.group(1 - near, far)

    def remote(src, dst, send_sem, recv_sem, target):
        pltpu.make_async_remote_copy(
            src_ref=src, dst_ref=dst, send_sem=send_sem, recv_sem=recv_sem, device_id=target, device_id_type=MESH
        ).start()

    def wait(ref, sem):
        pltpu.make_async_copy(ref, ref, sem).wait()

    def each(count, body):
        lax.fori_loop(0, count, lambda i, carry: (body(i), carry)[1], 0)

    def columns(p):
        width = rights[p].shape[1]
        return [(start, min(256, width - start)) for start in range(0, width, 256)]

    def terms(p, owner, group, add):
        rows = work[p].shape[1]
        first, source = group * depth, owner * (4 * depth) + group * depth
        if p >= dots:
            given = givens[p - dots]

            def one(i):
                if add:
                    total = given[source + i].astype(f32) + core_in[p][first + i].astype(f32)
                    work[p][first + i] = total.astype(work[p].dtype)
                else:
                    work[p][first + i] = given[source + i]

            each(depth, one)
        elif rows % 16:

            def one(i):
                left = lefts[p][source + i]
                for start, size in columns(p):
                    cols = slice(start, start + size)
                    total = jnp.dot(left, rights[p][:, cols], preferred_element_type=f32)
                    if add:
                        total = total + core_in[p][first + i, :, cols].astype(f32)
                    work[p][first + i, :, cols] = total.astype(work[p].dtype)

            each(depth, one)
        else:
            left = lefts[p][pl.ds(source, depth)].reshape(depth * rows, lefts[p].shape[2])
            for start, size in columns(p):
                cols = slice(start, start + size)
                total = jnp.dot(left, rights[p][:, cols], preferred_element_type=f32).reshape(depth, rows, size)
                if add:
                    total = total + core_in[p][pl.ds(first, depth), :, cols].astype(f32)
                work[p][pl.ds(first, depth), :, cols] = total.astype(work[p].dtype)

    def to_other_core(p):
        def one(group):
            terms(p, 1 - core, group, False)
            part = pl.ds(group * depth, depth)
            remote(work[p].at[part], core_in[p].at[part], core_out.at[p], core_got.at[p], to_core)

        each(4, one)

    def own_terms(p):
        wait(work[p], core_out.at[p])
        wait(core_in[p], core_got.at[p])

        def away(k):
            group = place.group((1 - near) * (1 - k) + near * k, 1 - far)
            terms(p, core, group, True)
            remote(
                work[p].at[pl.ds(group * depth, depth)],
                far_in[p].at[pl.ds(k * depth, depth)],
                far_out.at[p],
                far_got.at[k, p],
                to_far,
            )

        each(2, away)

        def home(k):
            terms(p, core, beside * (1 - k) + here * k, True)

        each(2, home)

    def to_beside(p):
        wait(far_in[p].at[pl.ds(0, depth)], far_got.at[0, p])

        def one(i):
            total = work[p][beside * depth + i].astype(f32) + far_in[p][i].astype(f32)
            work[p][beside * depth + i] = total.astype(work[p].dtype)

        each(depth, one)
        remote(work[p].at[pl.ds(beside * depth, depth)], near_in[p], near_out.at[p], near_got.at[p], to_near)

    def held(p, zb):
        return (
            work[p][here * depth + zb].astype(f32)
            + far_in[p][depth + zb].astype(f32)
            + near_in[p][zb].astype(f32)
        )

    def along(p):
        wait(far_in[p].at[pl.ds(depth, depth)], far_got.at[1, p])
        wait(near_in[p], near_got.at[p])

        def pass_on(zb, edge, landing, got, out, target):
            mine = work[p].at[here * depth + zb]

            @pl.when(edge)
            def _():
                mine[...] = held(p, zb).astype(work[p].dtype)

            @pl.when(jnp.logical_not(edge))
            def _():
                wait(landing[p].at[zb], got.at[zb, p])
                mine[...] = (held(p, zb) + landing[p][zb].astype(f32)).astype(work[p].dtype)

            remote(mine, landing[p].at[zb], out.at[zb, p], got.at[zb, p], target)

        def step(k):
            up, down = depth - 1 - k, k

            @pl.when(up > z)
            def _():
                pass_on(up, z == 0, up_in, up_got, up_out, above)

            @pl.when(down < z)
            def _():
                pass_on(down, z == depth - 1, down_in, down_got, down_out, below)

        each(depth, step)

    def finish(p):
        outs[p][...] = held(p, z)

        @pl.when(z > 0)
        def _():
            wait(up_in[p].at[z], up_got.at[z, p])
            outs[p][...] += up_in[p][z].astype(f32)

        @pl.when(z + 1 < depth)
        def _():
            wait(down_in[p].at[z], down_got.at[z, p])
            outs[p][...] += down_in[p][z].astype(f32)

    early = [to_other_core, own_terms]
    late = [to_beside, along, finish]
    for stages in (early, late):
        for tick in range(pieces + len(stages) - 1):
            for lag, stage in enumerate(stages):
                if 0 <= tick - lag < pieces:
                    stage(tick - lag)
    for p in range(pieces):
        wait(far_in[p], far_out.at[p])
        wait(near_in[p], near_out.at[p])

        def sent(zb):
            @pl.when(zb > z)
            def _():
                wait(up_in[p].at[zb], up_out.at[zb, p])

            @pl.when(zb < z)
            def _():
                wait(down_in[p].at[zb], down_out.at[zb, p])

        each(depth, sent)


def reduce_all(lefts, rights, givens, depth):
    dots, pieces = len(lefts), len(lefts) + len(givens)
    blocks = [(left.shape[1], right.shape[1], jnp.bfloat16) for left, right in zip(lefts, rights)]
    blocks += [given.shape[1:] + (given.dtype,) for given in givens]

    def buffers(count):
        return [pltpu.VMEM((count,) + block[:2], block[2]) for block in blocks]

    scratch = []
    for count in (4, 4, 2, 1, 1, 1):
        scratch += buffers(count * depth)
    sems = [(pieces,), (pieces,), (pieces,), (2, pieces), (pieces,), (pieces,)] + [(depth, pieces)] * 4
    return pl.pallas_call(
        functools.partial(reduce_kernel, depth, dots, pieces),
        out_shape=[jax.ShapeDtypeStruct(block[:2], jnp.float32) for block in blocks],
        in_specs=[pl.BlockSpec(memory_space=pltpu.VMEM)] * (2 * dots + len(givens)),
        out_specs=[pl.BlockSpec(memory_space=pltpu.VMEM)] * pieces,
        scratch_shapes=scratch + [pltpu.SemaphoreType.DMA(shape) for shape in sems],
        compiler_params=pltpu.CompilerParams(collective_id=1, has_side_effects=True, vmem_limit_bytes=67043328),
        name="reduce_all",
    )(*lefts, *rights, *givens)


def to_slots(values, depth):
    tail = values.shape[1:]
    split = values.reshape((depth, 2, 2, 2) + tail)
    order = (2, 1, 3, 0) + tuple(range(4, 4 + len(tail)))
    return jnp.transpose(split, order).reshape((8 * depth,) + tail)


def slot_order(rows, devices, held, depth):
    main = held // 8 * 8
    rest = held - main
    place = jnp.arange(rows, dtype=jnp.int32)
    owner, inner = place // held, place % held
    z, y, core, x = owner // 8, owner // 4 % 2, owner // 2 % 2, owner % 2
    slot = ((core * 2 + y) * 2 + x) * depth + z
    target = jnp.where(inner < main, slot * main + inner, devices * main + slot * rest + inner - main)
    return (target[:, None] == place[None, :]).astype(jnp.bfloat16)


def on_device_fast(depth, block_input, grad_output, segments, w_qkv, w_out, w_fc1, w_fc2, params):
    f32 = jnp.float32
    bf16 = jnp.bfloat16
    seqs, toks, width = block_input.shape
    seq_count = lax.axis_size("seq")
    seq_index = lax.axis_index("seq")
    devices = lax.axis_size(AXES)
    full_len = toks * seq_count
    count = seqs * toks
    held = piece_rows(w_out, width)
    main = held // 8 * 8
    rest = held - main
    wide = [w.reshape(held, -1) for w in (w_qkv, w_out, w_fc1)]
    widths = [w.shape[1] for w in wide]
    rest_rows = jnp.concatenate([w[main:] for w in wide], axis=1).reshape(8, -1)
    slots = -(-params.shape[1] // 1024) * 1024
    vec = jnp.pad(params, ((0, 0), (0, slots - params.shape[1]))).reshape(-1, 128)
    blocks = [w[:main] for w in wide] + [w_fc2.reshape(-1, width), rest_rows, vec]
    whole = gather_all(blocks, (False, False, False, True, False, True), depth)
    tops = [w.reshape(devices * main, -1) for w in whole[:3]]
    mat_fc2 = whole[3].reshape(-1, width)
    rests = whole[4].reshape(devices * rest, -1)
    mats = []
    start = 0
    for top, cols in zip(tops, widths):
        mats.append([top, rests[:, start : start + cols]])
        start += cols
    mat_qkv, mat_out, mat_fc1 = mats
    all_params = whole[5].reshape(devices, slots)[:, : params.shape[1]]
    order = slot_order(width, devices, held, depth)
    gain1, shift1, bias_q, bias_v, bias_o, gain2, shift2, bias_f1, bias_f2 = split_params(all_params)
    bias_qkv = jnp.concatenate([bias_q, jnp.zeros((width,), f32), bias_v])
    rows = block_input.reshape(count, width).astype(f32)
    h1f, normed1, inv1 = layer_norm(rows, gain1, shift1)
    h1 = reorder(h1f.astype(bf16), order)
    qkv = (times(h1, mat_qkv) + bias_qkv).astype(bf16)
    query = qkv[:, :width].reshape(seqs, toks, HEADS, HEAD_DIM)
    both = gather_seq(qkv[:, width:].reshape(seqs, toks, 2 * width))
    keys = both[:, :, :width].reshape(seqs, full_len, HEADS, HEAD_DIM)
    values = both[:, :, width:].reshape(seqs, full_len, HEADS, HEAD_DIM)
    offset = seq_index * toks
    query_place = offset + jnp.arange(toks, dtype=jnp.int32)
    key_place = jnp.arange(full_len, dtype=jnp.int32)
    query_segs = lax.dynamic_slice_in_dim(segments, offset, toks, 1)
    allowed = (query_segs[:, :, None] == segments[:, None, :]) & (
        key_place[None, None, :] <= query_place[None, :, None]
    )
    out, lse = attend_forward(query, keys, values, allowed)
    out_rows = reorder(out.reshape(count, width), order)
    resid = rows + times(out_rows, mat_out) + bias_o
    h2f, normed2, inv2 = layer_norm(resid, gain2, shift2)
    h2 = reorder(h2f.astype(bf16), order)
    upper = times(h2, mat_fc1) + bias_f1
    act = gelu_value(upper).astype(bf16)
    result = (resid + times(act, [mat_fc2]) + bias_f2).astype(bf16)
    cotangent = grad_output.reshape(count, width)
    cot_f = cotangent.astype(f32)
    d_bf2 = jnp.sum(cot_f, axis=0)
    d_upper = times_t(cotangent, [mat_fc2]) * gelu_slope(upper)
    d_bf1 = jnp.sum(d_upper, axis=0)
    d_upper_b = d_upper.astype(bf16)
    d_h2 = restore(times_t(d_upper_b, mat_fc1), order)
    d_gain2 = jnp.sum(d_h2 * normed2, axis=0)
    d_shift2 = jnp.sum(d_h2, axis=0)
    d_resid = cot_f + norm_back(d_h2, normed2, inv2, gain2)
    d_resid_b = d_resid.astype(bf16)
    d_bo = jnp.sum(d_resid, axis=0)
    d_attn = restore(times_t(d_resid_b, mat_out).astype(bf16), order)
    d_attn = d_attn.reshape(seqs, toks, HEADS, HEAD_DIM)
    dquery, dkeys_all, dvals_all = attend_back(query, keys, values, out, d_attn, lse, allowed)
    d_both = jnp.concatenate(
        [dkeys_all.reshape(seqs, full_len, width), dvals_all.reshape(seqs, full_len, width)], axis=2
    )
    d_both = scatter_seq(d_both).reshape(count, 2 * width)
    dquery = dquery.reshape(count, width)
    d_qkv_b = jnp.concatenate([dquery, d_both], axis=1).astype(bf16)
    d_bq = jnp.sum(dquery, axis=0)
    d_bv = jnp.sum(d_both[:, width:], axis=0)
    d_h1 = restore(times_t(d_qkv_b, mat_qkv), order)
    d_gain1 = jnp.sum(d_h1 * normed1, axis=0)
    d_shift1 = jnp.sum(d_h1, axis=0)
    d_input = d_resid + norm_back(d_h1, normed1, inv1, gain1)
    d_vec = jnp.concatenate([d_gain1, d_shift1, d_bq, d_bv, d_bo, d_gain2, d_shift2, d_bf1, d_bf2])
    d_vec = jnp.pad(d_vec.reshape(devices, -1), ((0, 0), (0, slots - params.shape[1])))
    lefts = [to_slots(act.T.reshape(devices, -1, count), depth)]
    lefts += [left[:, : devices * main].T.reshape(devices, main, count) for left in (h2, h1, out_rows)]
    rights = [cotangent, d_upper_b, d_qkv_b, d_resid_b]
    ends = [grad_block(left[:, devices * main :], right) for left, right in
            ((h1, d_qkv_b), (out_rows, d_resid_b), (h2, d_upper_b))]
    ends = jnp.concatenate(ends, axis=1).astype(bf16).reshape(devices, 8, -1)
    givens = [ends, to_slots(d_vec.reshape(devices, -1, 128), depth)]
    top_fc2, top_fc1, top_qkv, top_out, end_rows, end_vec = reduce_all(lefts, rights, givens, depth)
    end_rows = end_rows.reshape(rest, -1)
    grads = []
    start = 0
    for top in (top_qkv, top_out, top_fc1):
        cols = top.shape[1]
        grads.append(jnp.concatenate([top, end_rows[:, start : start + cols]], axis=0).reshape(1, -1))
        start += cols
    return (
        result.reshape(seqs, toks, width),
        d_input.reshape(seqs, toks, width),
        grads[0],
        grads[1],
        grads[2],
        top_fc2.reshape(1, -1),
        end_vec.reshape(1, -1)[:, : params.shape[1]],
    )


def on_device(block_input, grad_output, segments, w_qkv, w_out, w_fc1, w_fc2, params):
    f32 = jnp.float32
    seqs, toks, width = block_input.shape
    seq_count = lax.axis_size("seq")
    seq_index = lax.axis_index("seq")
    full_len = toks * seq_count
    count = seqs * toks
    mat_qkv, mat_out, mat_fc1, mat_fc2 = gather_matrices(
        (w_qkv, w_out, w_fc1, w_fc2),
        ((width, 3 * width), (width, width), (width, FF), (FF, width)),
        (False, True, False, True),
    )
    by_rows = piece_rows(w_out, width) > 0
    if by_rows:
        all_params = gather_by_doubling(params, False)
    else:
        all_params = lax.all_gather(params, AXES, axis=0, tiled=True)
    order = None
    held = piece_rows(w_out, width)
    if held:
        order = column_order(width, lax.axis_size(AXES), held)
    gain1, shift1, bias_q, bias_v, bias_o, gain2, shift2, bias_f1, bias_f2 = split_params(
        all_params
    )
    bias_qkv = jnp.concatenate([bias_q, jnp.zeros((width,), f32), bias_v])
    rows = block_input.reshape(count, width).astype(f32)
    h1f, normed1, inv1 = layer_norm(rows, gain1, shift1)
    h1 = h1f.astype(jnp.bfloat16)
    h1 = reorder(h1, order)
    qkv = (times(h1, mat_qkv) + bias_qkv).astype(jnp.bfloat16)
    query = qkv[:, :width].reshape(seqs, toks, HEADS, HEAD_DIM)
    both = gather_seq(qkv[:, width:].reshape(seqs, toks, 2 * width))
    keys = both[:, :, :width].reshape(seqs, full_len, HEADS, HEAD_DIM)
    values = both[:, :, width:].reshape(seqs, full_len, HEADS, HEAD_DIM)
    offset = seq_index * toks
    query_place = offset + jnp.arange(toks, dtype=jnp.int32)
    key_place = jnp.arange(full_len, dtype=jnp.int32)
    query_segs = lax.dynamic_slice_in_dim(segments, offset, toks, 1)
    allowed = (query_segs[:, :, None] == segments[:, None, :]) & (
        key_place[None, None, :] <= query_place[None, :, None]
    )
    out, lse = attend_forward(query, keys, values, allowed)
    out_rows = reorder(out.reshape(count, width), order)
    resid = rows + times(out_rows, mat_out) + bias_o
    h2f, normed2, inv2 = layer_norm(resid, gain2, shift2)
    h2 = reorder(h2f.astype(jnp.bfloat16), order)
    upper = times(h2, mat_fc1) + bias_f1
    act = gelu_value(upper).astype(jnp.bfloat16)
    result = (resid + times(act, mat_fc2) + bias_f2).astype(
        jnp.bfloat16
    )
    cotangent = grad_output.reshape(count, width)
    cot_f = cotangent.astype(f32)
    d_bf2 = jnp.sum(cot_f, axis=0)
    d_upper = times_t(cotangent, mat_fc2) * gelu_slope(upper)
    d_bf1 = jnp.sum(d_upper, axis=0)
    d_upper_b = d_upper.astype(jnp.bfloat16)
    pair_fc2 = scatter_grad(act, cotangent, mat_fc2, w_fc2, True)
    pair_fc1 = scatter_grad(h2, d_upper_b, mat_fc1, w_fc1, False)
    d_h2 = restore(times_t(d_upper_b, mat_fc1), order)
    d_gain2 = jnp.sum(d_h2 * normed2, axis=0)
    d_shift2 = jnp.sum(d_h2, axis=0)
    d_resid = cot_f + norm_back(d_h2, normed2, inv2, gain2)
    d_resid_b = d_resid.astype(jnp.bfloat16)
    d_bo = jnp.sum(d_resid, axis=0)
    pair_out = scatter_grad(out_rows, d_resid_b, mat_out, w_out, False)
    d_attn = restore(times_t(d_resid_b, mat_out).astype(jnp.bfloat16), order)
    d_attn = d_attn.reshape(seqs, toks, HEADS, HEAD_DIM)
    dquery, dkeys_all, dvals_all = attend_back(query, keys, values, out, d_attn, lse, allowed)
    d_both = jnp.concatenate(
        [
            dkeys_all.reshape(seqs, full_len, width),
            dvals_all.reshape(seqs, full_len, width),
        ],
        axis=2,
    )
    d_both = scatter_seq(d_both)
    d_both = d_both.reshape(count, 2 * width)
    dquery = dquery.reshape(count, width)
    dvals = d_both[:, width:]
    d_qkv_b = jnp.concatenate([dquery, d_both], axis=1).astype(jnp.bfloat16)
    d_bq = jnp.sum(dquery, axis=0)
    d_bv = jnp.sum(dvals, axis=0)
    d_h1 = restore(times_t(d_qkv_b, mat_qkv), order)
    d_gain1 = jnp.sum(d_h1 * normed1, axis=0)
    d_shift1 = jnp.sum(d_h1, axis=0)
    d_input = d_resid + norm_back(d_h1, normed1, inv1, gain1)
    d_vec = jnp.concatenate([d_gain1, d_shift1, d_bq, d_bv, d_bo, d_gain2, d_shift2, d_bf1, d_bf2])
    pair_qkv = scatter_grad(h1, d_qkv_b, mat_qkv, w_qkv, True)
    grad_qkv, grad_out, grad_fc1, grad_fc2 = finish_grads(
        (pair_qkv, pair_out, pair_fc1, pair_fc2), (w_qkv, w_out, w_fc1, w_fc2)
    )
    vec_rows = d_vec.reshape(-1, params.shape[1])
    if by_rows:
        grad_vec = sum_by_halves(vec_rows[:, None], False)
    else:
        grad_vec = lax.psum_scatter(vec_rows, AXES, scatter_dimension=0, tiled=True)
    return (
        result.reshape(seqs, toks, width),
        d_input.reshape(seqs, toks, width),
        grad_qkv,
        grad_out,
        grad_fc1,
        grad_fc2,
        grad_vec,
    )


def solution(mesh):
    placed = (
        P("dp", "seq", None),
        P("dp", "seq", None),
        P("dp", None),
        P(("dp", "seq"), None),
        P(("dp", "seq"), None),
        P(("dp", "seq"), None),
        P(("dp", "seq"), None),
        P(("dp", "seq"), None),
    )
    depth = mesh.shape["dp"] // 4

    def either(*args):
        shards = args[3:7]
        by_rows = piece_rows(shards[1], args[0].shape[2]) % 16 == 2
        if mesh.shape["seq"] == 2 and mesh.shape["dp"] == 4 * depth and by_rows:
            return on_device_fast(depth, *args)
        return on_device(*args)

    return jax.shard_map(
        either,
        mesh=mesh,
        in_specs=placed,
        out_specs=(
            P("dp", "seq", None),
            P("dp", "seq", None),
            P(("dp", "seq"), None),
            P(("dp", "seq"), None),
            P(("dp", "seq"), None),
            P(("dp", "seq"), None),
            P(("dp", "seq"), None),
        ),
        check_vma=False,
    )
```
